32 devices in a mesh: row: 4 (over x, core), col: 8 (over z, y).
Axes of the slice: x: 2, y: 2, z: 4, core: 2. Of those that a mesh axis runs over, the one named last changes fastest.
Arguments:
- amplitudes: bfloat16 [640, 90000], P(('row', 'col')), may hold values from -6 to 6
- coulomb: bfloat16 [90000, 8192], P('col', 'row'), may hold values from -0.01953125 to 0.01953125
Outputs:
- ladder: float32 [640, 8192], P('col', 'row')
The draws below stay inside these ranges and needn't reach their ends.
All inputs are finite; a program needn't handle non-finite values.
Results may differ from the reference program's by a relative error of at most 0.0003.
Values may be sent and summed in bfloat16 or wider, within the bound.
A program may use at most 192 MiB of HBM per device.

```python
import jax
import jax.numpy as jnp
from jax import lax

CD = 90000
IJ = 640
AB_DEV = 2048
AB = 8192
N_ROW = 4


def level_of(own_key, shape, cuts, smallest, high):
    def one(axis_at, parts):
        heights = jax.random.uniform(jax.random.fold_in(jax.random.fold_in(own_key, 6), axis_at), (parts,), jnp.float32, smallest / len(cuts), high / len(cuts))
        return jnp.repeat(jnp.exp(heights), shape[axis_at] // parts).reshape((-1,) + (1,) * (len(shape) - axis_at - 1))

    factor_of = one(*cuts[0])
    for cut in cuts[1:]:
        factor_of = factor_of * one(*cut)
    return factor_of


def bell_draw(key, dims, width, reach, shards=(), held_as=jnp.bfloat16):
    factor_of = level_of(key, dims, shards, -0.22, 0.18) if shards else 1.0
    result = jax.random.normal(key, dims, jnp.float32) * width * factor_of
    return jnp.minimum(jnp.maximum(result, -reach), reach).astype(held_as)


def setup_inputs(seed: int = 0) -> dict:
    seeds = jax.random.split(jax.random.key(seed), 3)
    amplitudes = bell_draw(seeds[0], (IJ, CD), 1.0, 6.0, ((0, 32),))
    coulomb = bell_draw(seeds[1], (CD, AB), CD ** -0.5, 0.01953125, ((0, 8), (1, 4)))
    return {"amplitudes": amplitudes, "coulomb": coulomb}


def reference(amplitudes, coulomb):
    left = amplitudes.astype(jnp.float32)
    blocks = []
    for index in range(N_ROW):
        slab_part = coulomb[:, index * AB_DEV:(index + 1) * AB_DEV].astype(jnp.float32)
        blocks.append(jnp.dot(left, slab_part, precision=lax.Precision.HIGHEST, preferred_element_type=jnp.float32))
    contraction = jnp.concatenate(blocks, axis=1)
    return 0.5 * contraction
```

```python
import jax
import jax.numpy as jnp
from jax import lax
from jax.sharding import PartitionSpec as P


def shards(amplitudes, coulomb):
    columns = lax.axis_size("col")
    grid_rows = lax.axis_size("row")
    pairs_here = amplitudes.shape[0]
    blocks = amplitudes.reshape(pairs_here, columns, -1).transpose(1, 0, 2)
    mine = lax.all_to_all(blocks, "col", split_axis=0, concat_axis=0, tiled=True)
    mine = mine.reshape(columns * pairs_here, -1)
    amp_panel = lax.all_gather(mine, "row", axis=0, tiled=True)
    contraction = lax.psum_scatter(
        jnp.dot(amp_panel, coulomb, preferred_element_type=jnp.float32),
        "col",
        scatter_dimension=0,
        tiled=True,
    )
    return 0.5 * contraction


def solution(mesh):
    return jax.shard_map(
        shards,
        mesh=mesh,
        in_specs=(P(("row", "col"), None), P("col", "row")),
        out_specs=P("col", "row"),
        check_vma=False,
    )
```

```python
import jax
import jax.numpy as jnp
from jax import lax
from jax.sharding import PartitionSpec as P


CD_CHUNKS = 3
AB_CHUNKS = 2
LANES = 128


def cuts(length, parts, unit):
    step = -(-(-(-length // unit)) // parts) * unit
    return [(at, min(at + step, length)) for at in range(0, length, step)]


def shards(amplitudes, coulomb):
    columns = lax.axis_size("col")
    pairs_here = amplitudes.shape[0]
    blocks = amplitudes.reshape(pairs_here, columns, -1).transpose(1, 0, 2)
    cd_cuts = cuts(coulomb.shape[0], CD_CHUNKS, LANES)
    ab_cuts = cuts(coulomb.shape[1], AB_CHUNKS, LANES)
    totals = [None] * len(ab_cuts)
    token = None
    for low, high in cd_cuts:
        piece = blocks[:, :, low:high]
        if token is not None:
            piece, token = lax.optimization_barrier((piece, token))
        mine = lax.all_to_all(piece, "col", split_axis=0, concat_axis=0, tiled=True)
        mine = mine.reshape(columns * pairs_here, -1)
        token = mine
        panel = lax.all_gather(mine, "row", axis=0, tiled=True)
        for at, (left, right) in enumerate(ab_cuts):
            term = jnp.dot(panel, coulomb[low:high, left:right], preferred_element_type=jnp.float32)
            total = term if totals[at] is None else totals[at] + term
            totals[at] = lax.optimization_barrier(total)
    out = [
        lax.psum_scatter(total, "col", scatter_dimension=0, tiled=True)
        for total in totals
    ]
    return 0.5 * jnp.concatenate(out, axis=1)


def solution(mesh):
    return jax.shard_map(
        shards,
        mesh=mesh,
        in_specs=(P(("row", "col"), None), P("col", "row")),
        out_specs=P("col", "row"),
        check_vma=False,
    )
```

```python
import jax
import jax.numpy as jnp
from jax import lax
from jax.sharding import PartitionSpec as P


CD_SHARES = (36, 31, 21)
LANES = 128


def cuts(length, shares, unit):
    tiles = -(-length // unit)
    edges = [tiles * sum(shares[:at]) // sum(shares) * unit for at in range(len(shares))]
    return list(zip(edges, edges[1:] + [length]))


def shards(amplitudes, coulomb):
    columns = lax.axis_size("col")
    pairs_here = amplitudes.shape[0]
    blocks = amplitudes.reshape(pairs_here, columns, -1).transpose(1, 0, 2)
    cd_cuts = cuts(coulomb.shape[0], CD_SHARES, LANES)
    total = None
    token = None
    for low, high in cd_cuts:
        piece = blocks[:, :, low:high]
        if token is not None:
            piece, token = lax.optimization_barrier((piece, token))
        mine = lax.all_to_all(piece, "col", split_axis=0, concat_axis=0, tiled=True)
        mine = mine.reshape(columns * pairs_here, -1)
        token = mine
        panel = lax.all_gather(mine, "row", axis=0, tiled=True)
        term = jnp.dot(panel, coulomb[low:high], preferred_element_type=jnp.float32)
        total = lax.optimization_barrier(term if total is None else total + term)
    return 0.5 * lax.psum_scatter(total, "col", scatter_dimension=0, tiled=True)


def solution(mesh):
    return jax.shard_map(
        shards,
        mesh=mesh,
        in_specs=(P(("row", "col"), None), P("col", "row")),
        out_specs=P("col", "row"),
        check_vma=False,
    )
```
